32 devices in a mesh: ens: 16 (over z, y, x), slab: 2 (over core).
Axes of the slice: x: 2, y: 2, z: 4, core: 2. Of those that a mesh axis runs over, the one named last changes fastest.
Arguments:
- ensemble: float32 [16, 3, 128, 768], P('ens', None, 'slab'), may hold values from -6 to 6
- perturbation: float32 [16, 3, 128, 768], P('ens', None, 'slab'), may hold values from -6 to 6
- ancestors: int32 [16], P('ens'), may hold values from 0 to 15
- bathymetry: int32 [128, 768], replicated, may hold values from 50 to 200
Outputs:
- analysis: float32 [16, 3, 128, 768], P('ens', None, 'slab')
The draws below stay inside these ranges and needn't reach their ends.
Inputs may be any that keep to these rules, and one draw needn't show every extreme that they name: `ancestors`: each entry names the old particle that a new particle copies.
All inputs are finite; a program needn't handle non-finite values.
Results may differ from the reference program's by a relative error of at most 0.00002.
Values sent between devices are 32-bit elements; how exact they have to be, the bound alone decides.
A program may use at most 128 MiB of HBM per device.

```python
import jax
import jax.numpy as jnp
from jax import lax

NX = 768
STEPS = 3
PARTICLES = 16
NY = 128


def place_ends(drawn, key, smallest, top_value):
    dims = drawn.shape
    spot = [jax.random.randint(jax.random.fold_in(key, axis), (), 0, dims[axis]) for axis in range(len(dims))]
    drawn = drawn.at[tuple(spot)].set(smallest)
    longest = dims.index(max(dims))
    spot[longest] = (spot[longest] + 1) % dims[longest]
    return drawn.at[tuple(spot)].set(top_value)


def shard_levels(rng, dims, shards, low, top_value):
    def one(axis_at, shards_of):
        steps = jax.random.uniform(jax.random.fold_in(jax.random.fold_in(rng, 6), axis_at), (shards_of,), jnp.float32, low / len(shards), top_value / len(shards))
        return jnp.repeat(jnp.exp(steps), dims[axis_at] // shards_of).reshape((-1,) + (1,) * (len(dims) - axis_at - 1))

    loudness = one(*shards[0])
    for cut in shards[1:]:
        loudness = loudness * one(*cut)
    return loudness


def noise(own_key, extent, scale, limit, split=(), dtype=jnp.bfloat16):
    array = jax.random.normal(own_key, extent, jnp.float32) * scale
    if len(split) > 0:
        array = shard_levels(own_key, extent, split, -0.22, 0.18) * array
    return jnp.clip(array, min=-limit, max=limit).astype(dtype)


def setup_inputs(seed: int = 0) -> dict:
    seeds = jax.random.split(jax.random.key(seed), 5)
    return {
        "ensemble": noise(seeds[0], (PARTICLES, 3, NY, NX), 1.0, 6.0, ((0, 16), (2, 2)), jnp.float32),
        "perturbation": noise(seeds[1], (PARTICLES, 3, NY, NX), 1.0, 6.0, ((0, 16), (2, 2)), jnp.float32),
        "ancestors": place_ends(jax.random.randint(seeds[2], (PARTICLES,), 0, PARTICLES), jax.random.fold_in(seeds[2], 1), 0, PARTICLES - 1).astype(jnp.int32),
        "bathymetry": place_ends(jax.random.randint(seeds[3], (NY, NX), 50, 201), jax.random.fold_in(seeds[3], 1), 50, 200).astype(jnp.int32),
    }


RATIO = 0.3
TURNING = 0.03
JITTER = 0.5


def eastward_difference(field):
    return (jnp.roll(field, -1, -1) - jnp.roll(field, 1, -1)) * 0.5


def northward_difference(field):
    padded = jnp.pad(field, ((1, 1), (0, 0)))
    return (padded[2:] - padded[:-2]) * 0.5


def integrate_forward(ensemble_member, ocean_floor):
    height, east_vel, north_vel = ensemble_member[0], ensemble_member[1], ensemble_member[2]
    for substep in range(STEPS):
        flux_east = ocean_floor * east_vel
        flux_north = ocean_floor * north_vel
        height = height - RATIO * (eastward_difference(flux_east) + northward_difference(flux_north))
        east_next = east_vel - RATIO * eastward_difference(height) + TURNING * north_vel
        north_next = north_vel - RATIO * northward_difference(height) - TURNING * east_vel
        east_vel, north_vel = east_next, north_next
    return jnp.stack([height, east_vel, north_vel])


def smoothed_noise(ensemble_member):
    padded = jnp.pad(ensemble_member, ((0, 0), (1, 1), (0, 0)))
    return (4.0 * ensemble_member + padded[:, 2:] + padded[:, :-2] + jnp.roll(ensemble_member, 1, -1) + jnp.roll(ensemble_member, -1, -1)) * 0.125


def reference(ensemble, perturbation, ancestors, bathymetry):
    ocean_floor = bathymetry.astype(jnp.float32) * 0.01
    predicted_state = lax.map(lambda ensemble_member: integrate_forward(ensemble_member, ocean_floor), ensemble)
    selected_parents = jnp.take(predicted_state, ancestors.astype(jnp.int32), axis=0)
    return selected_parents + JITTER * lax.map(smoothed_noise, perturbation)
```

```python
import functools

import jax
import jax.numpy as jnp
from jax import lax
from jax.experimental import pallas as pl
from jax.experimental.pallas import tpu as pltpu
from jax.sharding import PartitionSpec as P

STEPS = 3
MESH = pl.DeviceIdType.MESH
STRIP = 8
LANES = 128


RATIO = 0.3
TURNING = 0.03
JITTER = 0.5


def padded(cells, sides, width):
    for axis, dim in sides:
        count = lax.axis_size(axis)
        ends = count - 1
        head = lax.slice_in_dim(cells, 0, width, axis=dim)
        tail = lax.slice_in_dim(cells, cells.shape[dim] - width, cells.shape[dim], axis=dim)
        cells = jnp.concatenate(
            [
                lax.ppermute(tail, axis, [(i, (i + 1) % count) for i in range(ends)]),
                cells,
                lax.ppermute(head, axis, [((i + 1) % count, i) for i in range(ends)]),
            ],
            axis=dim,
        )
    return cells


def eastward_difference(field):
    return (jnp.roll(field, -1, -1) - jnp.roll(field, 1, -1)) * 0.5


def step_rows(height, east_vel, north_vel, ocean_floor, inside):
    flux_east = ocean_floor * east_vel
    flux_north = ocean_floor * north_vel
    height_next = height[1:-1] - RATIO * (
        eastward_difference(flux_east[1:-1]) + (flux_north[2:] - flux_north[:-2]) * 0.5
    )
    height_next = jnp.where(inside[1:-1], height_next, 0.0)
    east_next = (
        east_vel[2:-2] - RATIO * eastward_difference(height_next[1:-1]) + TURNING * north_vel[2:-2]
    )
    north_next = (
        north_vel[2:-2]
        - RATIO * (height_next[2:] - height_next[:-2]) * 0.5
        - TURNING * east_vel[2:-2]
    )
    kept = inside[2:-2]
    return (height_next[1:-1], jnp.where(kept, east_next, 0.0), jnp.where(kept, north_next, 0.0))


def edge_rows(members, depth):
    return jnp.stack(
        [jnp.concatenate([member[:depth], member[-depth:]], axis=0) for member in members]
    )


def attach_rims(members, rims, depth):
    return [
        jnp.concatenate([rims[k, :depth], members[k], rims[k, 3 * depth :]], axis=0)
        for k in range(len(members))
    ]


def pick_rows(portion, lineage):
    return jnp.take(portion, lineage, axis=0, mode="clip")


def shards(ensemble, perturbation, ancestors, bathymetry):
    row_count = ensemble.shape[2]
    col_count = ensemble.shape[3]
    total_rows = bathymetry.shape[0]
    first_row = lax.axis_index("slab") * row_count
    widest = 2 * STEPS
    seabed_all = jnp.pad(bathymetry.astype(jnp.float32) * 0.01, ((widest, widest), (0, 0)))
    members = [ensemble[0, 0], ensemble[0, 1], ensemble[0, 2]]
    ocean_floor = lax.dynamic_slice_in_dim(seabed_all, first_row + widest - 2, row_count + 2 * 2, 0)
    global_row = first_row - 2 + jnp.arange(row_count + 2 * 2, dtype=jnp.int32)
    inside = ((global_row >= 0) & (global_row < total_rows))[:, None]
    ocean_floor, inside = (ocean_floor, inside)
    for substep in range(STEPS):
        rims = padded(edge_rows(members, 2), (("slab", 1),), 2)
        widened = attach_rims(members, rims, 2)
        members = list(step_rows(widened[0], widened[1], widened[2], ocean_floor, inside))
    noise = [perturbation[0, 0], perturbation[0, 1], perturbation[0, 2]]
    noise_rims = padded(edge_rows(noise, 1), (("slab", 1),), 1)
    bordered = attach_rims(noise, noise_rims, 1)
    smoothed = jnp.stack(
        [
            (
                4.0 * cell[1:-1]
                + cell[2:]
                + cell[:-2]
                + jnp.roll(cell[1:-1], 1, -1)
                + jnp.roll(cell[1:-1], -1, -1)
            )
            * 0.125
            for cell in bordered
        ]
    )
    lineage = lax.all_gather(ancestors, "ens", axis=0, tiled=True)
    flattened = jnp.stack(members).reshape(1, 3, row_count * col_count)
    pieces = lax.all_to_all(flattened, "ens", split_axis=2, concat_axis=0, tiled=True)
    picked = pick_rows(pieces, lineage)
    returned = lax.all_to_all(picked, "ens", split_axis=0, concat_axis=2, tiled=True)
    selected_parents = returned.reshape(1, 3, row_count, col_count)
    return selected_parents + JITTER * smoothed[None]


def whole_wait(ref, sem):
    pltpu.make_async_copy(ref, ref, sem).wait()


def cycle_kernel(
    n, pair, rows, cols,
    ens_ref, pert_ref, anc_ref, bath_ref, out_ref,
    state, noise, sb, seam, seam_sb, bath_v, pieces0, pieces1, pieces2, picked, res, lin_v, lin_s,
    halo_send, halo_recv, lin_send, lin_recv, lin_local, loads,
    a_send, a_recv, b_send, b_recv,
):
    me = lax.axis_index("ens")
    s = lax.axis_index("slab")
    plane = pair * pair
    line = n // plane
    hubs = 2 * plane
    base = (line // 2 - 1) * plane
    z = me // plane
    y = me // pair % pair
    x = me % pair
    inward = 1 - 2 * (z // (line // 2))
    hub = jnp.logical_and(me >= base, me < base + hubs)
    pieces = (pieces0, pieces1, pieces2)
    top = STRIP
    bottom = STRIP + rows
    barrier = pltpu.get_barrier_semaphore()

    def on(level, k):
        return (level * pair + (y + k // pair) % pair) * pair + (x + k % pair) % pair

    @pl.when(hub)
    def _():
        def greet(t, carry):
            to = lax.rem(me + 1 + t, n)
            pl.semaphore_signal(barrier, inc=1, device_id={"ens": to}, device_id_type=MESH)
            return carry

        lax.fori_loop(0, n - 1, greet, 0)

    pl.semaphore_signal(barrier, inc=1, device_id={"slab": 1 - s}, device_id_type=MESH)

    inner = pl.multiple_of((1 - s) * (rows - 2 * STRIP), STRIP)
    fills = [
        pltpu.make_async_copy(src, dst, loads.at[i])
        for i, (src, dst) in enumerate(
            (
                (bath_ref.at[pl.ds(pl.multiple_of(s * (rows - STRIP), STRIP), rows + STRIP)], bath_v),
                (ens_ref, state.at[:, pl.ds(top, rows)]),
                (
                    ens_ref.at[:, pl.ds(inner, 2 * STRIP)],
                    seam.at[:, pl.ds(pl.multiple_of(s * STRIP, STRIP), 2 * STRIP)],
                ),
                (pert_ref, noise.at[:, pl.ds(top, rows)]),
            )
        )
    ]
    for fill in fills:
        fill.start()

    lin_v[me] = jnp.full((1, LANES), anc_ref[0], jnp.int32)
    zeros = jnp.zeros((STRIP, cols), jnp.float32)
    for r in (0, bottom):
        sb[r : r + STRIP] = zeros
        for f in range(3):
            state[f, r : r + STRIP] = zeros
    fills[0].wait()
    for r in range(0, rows, STRIP):
        depth = bath_v[pl.ds(pl.multiple_of(s * STRIP + r, STRIP), STRIP)]
        sb[top + r : top + r + STRIP] = depth.astype(jnp.float32) * 0.01
    for r in range(0, 3 * STRIP, STRIP):
        depth = bath_v[pl.ds(pl.multiple_of((1 - s) * (rows - 2 * STRIP) + r, STRIP), STRIP)]
        seam_sb[r : r + STRIP] = depth.astype(jnp.float32) * 0.01
    fills[1].wait()
    fills[2].wait()

    def east(x):
        return (pltpu.roll(x, cols - 1, 1) - pltpu.roll(x, 1, 1)) * 0.5

    def shifted(ref, r, by):
        if 0 <= r + by <= ref.shape[0] - STRIP:
            return ref[r + by : r + by + STRIP]
        return pltpu.roll(ref[r : r + STRIP], -by % STRIP, 0)

    def heights(cells, floor, r):
        here = slice(r, r + STRIP)
        v = cells.at[2]
        northward = shifted(floor, r, 1) * shifted(v, r, 1) - shifted(floor, r, -1) * shifted(v, r, -1)
        eastward = east(floor[here] * cells[1, here])
        cells[0, here] = cells[0, here] - RATIO * (eastward + northward * 0.5)

    def velocities(cells, r):
        here = slice(r, r + STRIP)
        u = cells[1, here]
        v = cells[2, here]
        h = cells.at[0]
        cells[1, here] = u - RATIO * east(h[here]) + TURNING * v
        northward = (shifted(h, r, 1) - shifted(h, r, -1)) * 0.5
        cells[2, here] = v - RATIO * northward - TURNING * u

    for step in range(STEPS):
        for r in range(top, bottom, STRIP):
            heights(state, sb, r)
        for r in range(top, bottom, STRIP):
            velocities(state, r)

    edge = pl.multiple_of((1 - s) * (rows - STRIP), STRIP)

    def strip(ref, f, q, offset):
        return ref.at[f, pl.ds(pl.multiple_of(offset + (q + s * (hubs - 1 - 2 * q)) * STRIP, STRIP), STRIP)]

    def deliver(f, to):
        pltpu.make_async_remote_copy(
            src_ref=strip(state, f, to - base, top),
            dst_ref=pieces[f].at[me],
            send_sem=a_send.at[f],
            recv_sem=a_recv.at[f],
            device_id={"ens": to},
            device_id_type=MESH,
        ).start()

    def keep(f):
        pltpu.make_async_copy(strip(state, f, me - base, top), pieces[f].at[me], a_recv.at[f]).start()

    def tell(to):
        pltpu.make_async_remote_copy(
            src_ref=lin_v.at[me],
            dst_ref=lin_v.at[me],
            send_sem=lin_send,
            recv_sem=lin_recv,
            device_id={"ens": to},
            device_id_type=MESH,
        ).start()

    side = line // 2 - 1 + z // (line // 2)
    targets = [on(side + inward, k) for k in reversed(range(plane))]
    targets += [on(side, k) for k in reversed(range(plane))]
    last_hub = base + hubs - 1

    def away(f):
        for to in targets[:-1]:
            pl.when(to != last_hub)(lambda to=to: deliver(f, to))
        to = targets[-1]
        pl.when(jnp.logical_and(jnp.logical_not(hub), to != last_hub))(lambda: deliver(f, to))
        pl.when(jnp.logical_and(hub, to != last_hub))(lambda: keep(f))

    def seamed(f):
        pl.when(me != last_hub)(lambda: deliver(f, last_hub))
        pl.when(me == last_hub)(lambda: keep(f))

    pl.semaphore_wait(barrier, hubs + 1 - hub.astype(jnp.int32))
    halos = []
    for i, (src, dst, row) in enumerate(
        ((ens_ref, seam, s * 2 * STRIP), (pert_ref, noise, s * (rows + STRIP)))
    ):
        copy = pltpu.make_async_remote_copy(
            src_ref=src.at[:, pl.ds(edge, STRIP)],
            dst_ref=dst.at[:, pl.ds(pl.multiple_of(row, STRIP), STRIP)],
            send_sem=halo_send.at[i],
            recv_sem=halo_recv.at[i],
            device_id={"slab": 1 - s},
            device_id_type=MESH,
        )
        copy.start()
        halos.append(copy)
    for to in targets[:-1]:
        tell(to)
    pl.when(jnp.logical_not(hub))(lambda: tell(targets[-1]))
    away(0)
    halos[0].wait()
    for step in range(STEPS):
        last = step == STEPS - 1
        for r in range(0, 3 * STRIP, STRIP):
            heights(seam, seam_sb, r)
        for r in range(STRIP, 2 * STRIP, STRIP) if last else range(0, 3 * STRIP, STRIP):
            velocities(seam, r)
    for f in range(3):
        state[f, pl.ds(pl.multiple_of(top + edge, STRIP), STRIP)] = seam[f, STRIP : 2 * STRIP]

    seamed(0)
    for f in (1, 2):
        away(f)
        seamed(f)

    wall = pl.multiple_of(s * (rows + STRIP), STRIP)
    for f in range(3):
        noise[f, pl.ds(wall, STRIP)] = zeros
    fills[3].wait()
    halos[1].wait()
    for f in range(3):
        for r in range(top, bottom, STRIP):
            p = noise[f, r : r + STRIP]
            around = noise[f, r + 1 : r + 1 + STRIP] + noise[f, r - 1 : r - 1 + STRIP]
            total = 4.0 * p + around + pltpu.roll(p, 1, 1) + pltpu.roll(p, cols - 1, 1)
            out_ref[f, r - top : r - top + STRIP] = total * 0.125 * JITTER

    order = [t for t in range(line // 2, -(line // 2), -1) if t] + [0]
    spots = [(t, k) for t in order for k in reversed(range(plane))][: n - 1]

    def serve():
        whole_wait(lin_v.at[pl.ds(0, n - 1)], lin_recv)
        fetch = pltpu.make_async_copy(lin_v, lin_s, lin_local)
        fetch.start()
        fetch.wait()

        def reply(f, i):
            t, k = spots[i]
            to = on(z + t * inward, k)
            picked[f, i] = pieces[f][lin_s[to, 0, 0]]
            pltpu.make_async_remote_copy(
                src_ref=picked.at[f, i],
                dst_ref=strip(res, f, me - base, 0),
                send_sem=b_send.at[f],
                recv_sem=b_recv.at[f],
                device_id={"ens": to},
                device_id_type=MESH,
            ).start()

        for stage in range(3 + line // 2 - 1):
            if stage < 3:
                whole_wait(pieces[stage], a_recv.at[stage])
            for i, (t, k) in enumerate(spots):
                f = stage - max(line // 2 - t, 0) if t > 0 else stage
                if 0 <= f < 3:
                    reply(f, i)
            if stage < 3:
                picked[stage, n - 1] = pieces[stage][lin_s[me, 0, 0]]
                pltpu.make_async_copy(
                    picked.at[stage, n - 1], strip(res, stage, me - base, 0), b_recv.at[stage]
                ).start()

    pl.when(hub)(serve)

    for f in range(3):
        whole_wait(res.at[f], b_recv.at[f])
        for r in range(0, rows, STRIP):
            out_ref[f, r : r + STRIP] = res[f, r : r + STRIP] + out_ref[f, r : r + STRIP]

    @pl.when(hub)
    def _():
        whole_wait(lin_v.at[pl.ds(0, hubs - 1)], lin_send)
        for f in range(3):
            whole_wait(pieces[f].at[pl.ds(0, hubs - 1)], a_send.at[f])
            whole_wait(picked.at[f, pl.ds(0, n - 1)], b_send.at[f])

    @pl.when(jnp.logical_not(hub))
    def _():
        whole_wait(lin_v.at[pl.ds(0, hubs)], lin_send)
        for f in range(3):
            whole_wait(pieces[f].at[pl.ds(0, hubs)], a_send.at[f])


def cycle(n, pair, ensemble, perturbation, ancestors, bathymetry):
    rows, cols = ensemble.shape[2:]
    tall = rows + 2 * STRIP
    f32 = jnp.float32
    vmem = pl.BlockSpec(memory_space=pltpu.VMEM)
    hbm = pl.BlockSpec(memory_space=pltpu.HBM)
    dma = pltpu.SemaphoreType.DMA
    held = [
        pltpu.with_memory_space_constraint(x, pltpu.HBM)
        for x in (ensemble[0], perturbation[0], bathymetry)
    ]
    result = pl.pallas_call(
        functools.partial(cycle_kernel, n, pair, rows, cols),
        out_shape=jax.ShapeDtypeStruct((3, rows, cols), f32),
        in_specs=[hbm, hbm, pl.BlockSpec(memory_space=pltpu.SMEM), hbm],
        out_specs=vmem,
        scratch_shapes=[
            pltpu.VMEM((3, tall, cols), f32),
            pltpu.VMEM((3, tall, cols), f32),
            pltpu.VMEM((tall, cols), f32),
            pltpu.VMEM((3, 3 * STRIP, cols), f32),
            pltpu.VMEM((3 * STRIP, cols), f32),
            pltpu.VMEM((rows + STRIP, cols), jnp.int32),
            pltpu.VMEM((n, STRIP, cols), f32),
            pltpu.VMEM((n, STRIP, cols), f32),
            pltpu.VMEM((n, STRIP, cols), f32),
            pltpu.VMEM((3, n, STRIP, cols), f32),
            pltpu.VMEM((3, rows, cols), f32),
            pltpu.VMEM((n, 1, LANES), jnp.int32),
            pltpu.SMEM((n, 1, LANES), jnp.int32),
            dma((2,)), dma((2,)), dma(()), dma(()), dma(()), dma((4,)),
            dma((3,)), dma((3,)), dma((3,)), dma((3,)),
        ],
        compiler_params=pltpu.CompilerParams(collective_id=0, has_side_effects=True, vmem_limit_bytes=24 << 20),
        name="cycle",
    )(*held[:2], ancestors, held[2])
    return result[None]


def fits(mesh, ensemble):
    n, slabs = mesh.shape["ens"], mesh.shape["slab"]
    plane = slabs * slabs
    rows, cols = ensemble.shape[2] // slabs, ensemble.shape[3]
    if slabs != 2 or ensemble.shape[0] != n or n != plane * plane:
        return False
    return rows == 2 * plane * STRIP and cols % LANES == 0


def solution(mesh):
    in_specs = (P("ens", None, "slab", None), P("ens", None, "slab", None), P("ens"), P())
    out_specs = P("ens", None, "slab", None)

    def run(ensemble, perturbation, ancestors, bathymetry):
        body = functools.partial(cycle, mesh.shape["ens"], mesh.shape["slab"]) if fits(mesh, ensemble) else shards
        mapped = jax.shard_map(body, mesh=mesh, in_specs=in_specs, out_specs=out_specs, check_vma=False)
        return mapped(ensemble, perturbation, ancestors, bathymetry)

    return run
```

```python
import functools

import jax
import jax.numpy as jnp
from jax import lax
from jax.experimental import pallas as pl
from jax.experimental.pallas import tpu as pltpu
from jax.sharding import PartitionSpec as P

STEPS = 3
MESH = pl.DeviceIdType.MESH
STRIP = 8
LANES = 128


RATIO = 0.3
TURNING = 0.03
JITTER = 0.5


def padded(cells, sides, width):
    for axis, dim in sides:
        count = lax.axis_size(axis)
        ends = count - 1
        head = lax.slice_in_dim(cells, 0, width, axis=dim)
        tail = lax.slice_in_dim(cells, cells.shape[dim] - width, cells.shape[dim], axis=dim)
        cells = jnp.concatenate(
            [
                lax.ppermute(tail, axis, [(i, (i + 1) % count) for i in range(ends)]),
                cells,
                lax.ppermute(head, axis, [((i + 1) % count, i) for i in range(ends)]),
            ],
            axis=dim,
        )
    return cells


def eastward_difference(field):
    return (jnp.roll(field, -1, -1) - jnp.roll(field, 1, -1)) * 0.5


def step_rows(height, east_vel, north_vel, ocean_floor, inside):
    flux_east = ocean_floor * east_vel
    flux_north = ocean_floor * north_vel
    height_next = height[1:-1] - RATIO * (
        eastward_difference(flux_east[1:-1]) + (flux_north[2:] - flux_north[:-2]) * 0.5
    )
    height_next = jnp.where(inside[1:-1], height_next, 0.0)
    east_next = (
        east_vel[2:-2] - RATIO * eastward_difference(height_next[1:-1]) + TURNING * north_vel[2:-2]
    )
    north_next = (
        north_vel[2:-2]
        - RATIO * (height_next[2:] - height_next[:-2]) * 0.5
        - TURNING * east_vel[2:-2]
    )
    kept = inside[2:-2]
    return (height_next[1:-1], jnp.where(kept, east_next, 0.0), jnp.where(kept, north_next, 0.0))


def edge_rows(members, depth):
    return jnp.stack(
        [jnp.concatenate([member[:depth], member[-depth:]], axis=0) for member in members]
    )


def attach_rims(members, rims, depth):
    return [
        jnp.concatenate([rims[k, :depth], members[k], rims[k, 3 * depth :]], axis=0)
        for k in range(len(members))
    ]


def pick_rows(portion, lineage):
    return jnp.take(portion, lineage, axis=0, mode="clip")


def shards(ensemble, perturbation, ancestors, bathymetry):
    row_count = ensemble.shape[2]
    col_count = ensemble.shape[3]
    total_rows = bathymetry.shape[0]
    first_row = lax.axis_index("slab") * row_count
    widest = 2 * STEPS
    seabed_all = jnp.pad(bathymetry.astype(jnp.float32) * 0.01, ((widest, widest), (0, 0)))
    members = [ensemble[0, 0], ensemble[0, 1], ensemble[0, 2]]
    ocean_floor = lax.dynamic_slice_in_dim(seabed_all, first_row + widest - 2, row_count + 2 * 2, 0)
    global_row = first_row - 2 + jnp.arange(row_count + 2 * 2, dtype=jnp.int32)
    inside = ((global_row >= 0) & (global_row < total_rows))[:, None]
    ocean_floor, inside = (ocean_floor, inside)
    for substep in range(STEPS):
        rims = padded(edge_rows(members, 2), (("slab", 1),), 2)
        widened = attach_rims(members, rims, 2)
        members = list(step_rows(widened[0], widened[1], widened[2], ocean_floor, inside))
    noise = [perturbation[0, 0], perturbation[0, 1], perturbation[0, 2]]
    noise_rims = padded(edge_rows(noise, 1), (("slab", 1),), 1)
    bordered = attach_rims(noise, noise_rims, 1)
    smoothed = jnp.stack(
        [
            (
                4.0 * cell[1:-1]
                + cell[2:]
                + cell[:-2]
                + jnp.roll(cell[1:-1], 1, -1)
                + jnp.roll(cell[1:-1], -1, -1)
            )
            * 0.125
            for cell in bordered
        ]
    )
    lineage = lax.all_gather(ancestors, "ens", axis=0, tiled=True)
    flattened = jnp.stack(members).reshape(1, 3, row_count * col_count)
    pieces = lax.all_to_all(flattened, "ens", split_axis=2, concat_axis=0, tiled=True)
    picked = pick_rows(pieces, lineage)
    returned = lax.all_to_all(picked, "ens", split_axis=0, concat_axis=2, tiled=True)
    selected_parents = returned.reshape(1, 3, row_count, col_count)
    return selected_parents + JITTER * smoothed[None]


def whole_wait(ref, sem):
    pltpu.make_async_copy(ref, ref, sem).wait()


def cycle_kernel(
    n, pair, rows, cols,
    ens_ref, pert_ref, anc_ref, bath_ref, out_ref,
    state, noise, sb, seam, seam_sb, bath_v, pieces0, pieces1, pieces2, picked, res, lin_v, lin_s,
    halo_send, halo_recv, lin_send, lin_recv, lin_local, loads,
    a_send, a_recv, b_send, b_recv,
):
    me = lax.axis_index("ens")
    s = lax.axis_index("slab")
    plane = pair * pair
    line = n // plane
    hubs = 2 * plane
    base = (line // 2 - 1) * plane
    z = me // plane
    y = me // pair % pair
    x = me % pair
    inward = 1 - 2 * (z // (line // 2))
    hub = jnp.logical_and(me >= base, me < base + hubs)
    pieces = (pieces0, pieces1, pieces2)
    top = STRIP
    bottom = STRIP + rows
    barrier = pltpu.get_barrier_semaphore()

    def on(level, k):
        return (level * pair + (y + k // pair) % pair) * pair + (x + k % pair) % pair

    inner = pl.multiple_of((1 - s) * (rows - 2 * STRIP), STRIP)
    fills = [
        pltpu.make_async_copy(src, dst, loads.at[i])
        for i, (src, dst) in enumerate(
            (
                (bath_ref.at[pl.ds(pl.multiple_of(s * (rows - STRIP), STRIP), rows + STRIP)], bath_v),
                (ens_ref, state.at[:, pl.ds(top, rows)]),
                (
                    ens_ref.at[:, pl.ds(inner, 2 * STRIP)],
                    seam.at[:, pl.ds(pl.multiple_of(s * STRIP, STRIP), 2 * STRIP)],
                ),
                (pert_ref, noise.at[:, pl.ds(top, rows)]),
            )
        )
    ]
    for fill in fills:
        fill.start()
    @pl.when(hub)
    def _():
        def greet(t, carry):
            to = lax.rem(me + n - 1 - t, n)
            pl.semaphore_signal(barrier, inc=1, device_id={"ens": to}, device_id_type=MESH)
            return carry

        lax.fori_loop(0, n - 1, greet, 0)

    pl.semaphore_signal(barrier, inc=1, device_id={"slab": 1 - s}, device_id_type=MESH)


    lin_v[me] = jnp.full((1, LANES), anc_ref[0], jnp.int32)
    zeros = jnp.zeros((STRIP, cols), jnp.float32)
    for r in (0, bottom):
        sb[r : r + STRIP] = zeros
        for f in range(3):
            state[f, r : r + STRIP] = zeros
    fills[0].wait()
    for r in range(0, rows, STRIP):
        depth = bath_v[pl.ds(pl.multiple_of(s * STRIP + r, STRIP), STRIP)]
        sb[top + r : top + r + STRIP] = depth.astype(jnp.float32) * 0.01
    for r in range(0, 3 * STRIP, STRIP):
        depth = bath_v[pl.ds(pl.multiple_of((1 - s) * (rows - 2 * STRIP) + r, STRIP), STRIP)]
        seam_sb[r : r + STRIP] = depth.astype(jnp.float32) * 0.01
    fills[1].wait()
    fills[2].wait()

    def east(x):
        return (pltpu.roll(x, cols - 1, 1) - pltpu.roll(x, 1, 1)) * 0.5

    def shifted(ref, r, by):
        if 0 <= r + by <= ref.shape[0] - STRIP:
            return ref[r + by : r + by + STRIP]
        return pltpu.roll(ref[r : r + STRIP], -by % STRIP, 0)

    def heights(cells, floor, r):
        here = slice(r, r + STRIP)
        v = cells.at[2]
        northward = shifted(floor, r, 1) * shifted(v, r, 1) - shifted(floor, r, -1) * shifted(v, r, -1)
        eastward = east(floor[here] * cells[1, here])
        cells[0, here] = cells[0, here] - RATIO * (eastward + northward * 0.5)

    def velocities(cells, r):
        here = slice(r, r + STRIP)
        u = cells[1, here]
        v = cells[2, here]
        h = cells.at[0]
        cells[1, here] = u - RATIO * east(h[here]) + TURNING * v
        northward = (shifted(h, r, 1) - shifted(h, r, -1)) * 0.5
        cells[2, here] = v - RATIO * northward - TURNING * u

    def sweep(first, past):
        for wave in range(first, past):
            for step in range(STEPS):
                r = top + (wave - 2 * step) * STRIP
                if top <= r < bottom:
                    heights(state, sb, r)
                if top <= r - STRIP < bottom:
                    velocities(state, r - STRIP)

    half = plane + 2 * (STEPS - 1)
    early = z >= line // 2
    sweep(0, half)
    pl.when(jnp.logical_not(early))(lambda: sweep(half, half + plane + 1))

    edge = pl.multiple_of((1 - s) * (rows - STRIP), STRIP)

    def strip(ref, f, q, offset):
        return ref.at[f, pl.ds(pl.multiple_of(offset + q * STRIP, STRIP), STRIP)]

    def deliver(f, to):
        pltpu.make_async_remote_copy(
            src_ref=strip(state, f, to - base, top),
            dst_ref=pieces[f].at[me],
            send_sem=a_send.at[f],
            recv_sem=a_recv.at[f],
            device_id={"ens": to},
            device_id_type=MESH,
        ).start()

    def keep(f):
        pltpu.make_async_copy(strip(state, f, me - base, top), pieces[f].at[me], a_recv.at[f]).start()

    def tell(to):
        pltpu.make_async_remote_copy(
            src_ref=lin_v.at[me],
            dst_ref=lin_v.at[me],
            send_sem=lin_send,
            recv_sem=lin_recv,
            device_id={"ens": to},
            device_id_type=MESH,
        ).start()

    side = line // 2 - 1 + z // (line // 2)
    targets = [on(side + inward, k) for k in reversed(range(plane))]
    targets += [on(side, k) for k in reversed(range(plane))]
    seam_hub = base + (1 - s) * (hubs - 1)

    def across(f):
        for to in targets[:plane]:
            pl.when(to != seam_hub)(lambda to=to: deliver(f, to))

    def along(f):
        for to in targets[plane:-1]:
            pl.when(to != seam_hub)(lambda to=to: deliver(f, to))
        to = targets[-1]
        pl.when(jnp.logical_and(jnp.logical_not(hub), to != seam_hub))(lambda: deliver(f, to))
        pl.when(jnp.logical_and(hub, to != seam_hub))(lambda: keep(f))

    def seamed(f):
        pl.when(me != seam_hub)(lambda: deliver(f, seam_hub))
        pl.when(me == seam_hub)(lambda: keep(f))

    pl.semaphore_wait(barrier, hubs + 1 - hub.astype(jnp.int32))
    halos = []
    for i, (src, dst, row) in enumerate(
        ((ens_ref, seam, s * 2 * STRIP), (pert_ref, noise, s * (rows + STRIP)))
    ):
        copy = pltpu.make_async_remote_copy(
            src_ref=src.at[:, pl.ds(edge, STRIP)],
            dst_ref=dst.at[:, pl.ds(pl.multiple_of(row, STRIP), STRIP)],
            send_sem=halo_send.at[i],
            recv_sem=halo_recv.at[i],
            device_id={"slab": 1 - s},
            device_id_type=MESH,
        )
        copy.start()
        halos.append(copy)
    for to in targets[:-1]:
        tell(to)
    pl.when(jnp.logical_not(hub))(lambda: tell(targets[-1]))
    @pl.when(early)
    def _():
        across(0)
        sweep(half, half + plane + 1)

    pl.when(jnp.logical_not(early))(lambda: across(0))
    along(0)
    halos[0].wait()
    for step in range(STEPS):
        last = step == STEPS - 1
        for r in range(0, 3 * STRIP, STRIP):
            heights(seam, seam_sb, r)
        for r in range(STRIP, 2 * STRIP, STRIP) if last else range(0, 3 * STRIP, STRIP):
            velocities(seam, r)
    for f in range(3):
        state[f, pl.ds(pl.multiple_of(top + edge, STRIP), STRIP)] = seam[f, STRIP : 2 * STRIP]

    seamed(0)
    for f in (1, 2):
        pl.when(s == 0)(lambda f=f: across(f))
        along(f)
        pl.when(s == 1)(lambda f=f: across(f))
        seamed(f)

    wall = pl.multiple_of(s * (rows + STRIP), STRIP)
    for f in range(3):
        noise[f, pl.ds(wall, STRIP)] = zeros
    fills[3].wait()
    halos[1].wait()
    for f in range(3):
        for r in range(top, bottom, STRIP):
            p = noise[f, r : r + STRIP]
            around = noise[f, r + 1 : r + 1 + STRIP] + noise[f, r - 1 : r - 1 + STRIP]
            total = 4.0 * p + around + pltpu.roll(p, 1, 1) + pltpu.roll(p, cols - 1, 1)
            out_ref[f, r - top : r - top + STRIP] = total * 0.125 * JITTER

    order = [t for t in range(line // 2, -(line // 2), -1) if t] + [0]
    spots = [(t, k) for t in order for k in reversed(range(plane))][: n - 1]

    def serve():
        whole_wait(lin_v.at[pl.ds(0, n - 1)], lin_recv)
        fetch = pltpu.make_async_copy(lin_v, lin_s, lin_local)
        fetch.start()
        fetch.wait()

        def reply(f, i):
            t, k = spots[i]
            to = on(z + t * inward, k)
            picked[f, i] = pieces[f][lin_s[to, 0, 0]]
            pltpu.make_async_remote_copy(
                src_ref=picked.at[f, i],
                dst_ref=strip(res, f, me - base, 0),
                send_sem=b_send.at[f],
                recv_sem=b_recv.at[f],
                device_id={"ens": to},
                device_id_type=MESH,
            ).start()

        for stage in range(3 + line // 2 - 1):
            if stage < 3:
                whole_wait(pieces[stage], a_recv.at[stage])
            for i, (t, k) in enumerate(spots):
                f = stage - max(line // 2 - t, 0) if t > 0 else stage
                if 0 <= f < 3:
                    reply(f, i)
            if stage < 3:
                picked[stage, n - 1] = pieces[stage][lin_s[me, 0, 0]]
                pltpu.make_async_copy(
                    picked.at[stage, n - 1], strip(res, stage, me - base, 0), b_recv.at[stage]
                ).start()

    pl.when(hub)(serve)

    for f in range(3):
        whole_wait(res.at[f], b_recv.at[f])
        for r in range(0, rows, STRIP):
            out_ref[f, r : r + STRIP] = res[f, r : r + STRIP] + out_ref[f, r : r + STRIP]

    @pl.when(hub)
    def _():
        whole_wait(lin_v.at[pl.ds(0, hubs - 1)], lin_send)
        for f in range(3):
            whole_wait(pieces[f].at[pl.ds(0, hubs - 1)], a_send.at[f])
            whole_wait(picked.at[f, pl.ds(0, n - 1)], b_send.at[f])

    @pl.when(jnp.logical_not(hub))
    def _():
        whole_wait(lin_v.at[pl.ds(0, hubs)], lin_send)
        for f in range(3):
            whole_wait(pieces[f].at[pl.ds(0, hubs)], a_send.at[f])


def cycle(n, pair, ensemble, perturbation, ancestors, bathymetry):
    rows, cols = ensemble.shape[2:]
    tall = rows + 2 * STRIP
    f32 = jnp.float32
    vmem = pl.BlockSpec(memory_space=pltpu.VMEM)
    hbm = pl.BlockSpec(memory_space=pltpu.HBM)
    dma = pltpu.SemaphoreType.DMA
    held = [
        pltpu.with_memory_space_constraint(x, pltpu.HBM)
        for x in (ensemble[0], perturbation[0], bathymetry)
    ]
    result = pl.pallas_call(
        functools.partial(cycle_kernel, n, pair, rows, cols),
        out_shape=jax.ShapeDtypeStruct((3, rows, cols), f32),
        in_specs=[hbm, hbm, pl.BlockSpec(memory_space=pltpu.SMEM), hbm],
        out_specs=vmem,
        scratch_shapes=[
            pltpu.VMEM((3, tall, cols), f32),
            pltpu.VMEM((3, tall, cols), f32),
            pltpu.VMEM((tall, cols), f32),
            pltpu.VMEM((3, 3 * STRIP, cols), f32),
            pltpu.VMEM((3 * STRIP, cols), f32),
            pltpu.VMEM((rows + STRIP, cols), jnp.int32),
            pltpu.VMEM((n, STRIP, cols), f32),
            pltpu.VMEM((n, STRIP, cols), f32),
            pltpu.VMEM((n, STRIP, cols), f32),
            pltpu.VMEM((3, n, STRIP, cols), f32),
            pltpu.VMEM((3, rows, cols), f32),
            pltpu.VMEM((n, 1, LANES), jnp.int32),
            pltpu.SMEM((n, 1, LANES), jnp.int32),
            dma((2,)), dma((2,)), dma(()), dma(()), dma(()), dma((4,)),
            dma((3,)), dma((3,)), dma((3,)), dma((3,)),
        ],
        compiler_params=pltpu.CompilerParams(collective_id=0, has_side_effects=True, vmem_limit_bytes=24 << 20),
        name="cycle",
    )(*held[:2], ancestors, held[2])
    return result[None]


def fits(mesh, ensemble):
    n, slabs = mesh.shape["ens"], mesh.shape["slab"]
    plane = slabs * slabs
    rows, cols = ensemble.shape[2] // slabs, ensemble.shape[3]
    if slabs != 2 or ensemble.shape[0] != n or n != plane * plane:
        return False
    return rows == 2 * plane * STRIP and cols % LANES == 0


def solution(mesh):
    in_specs = (P("ens", None, "slab", None), P("ens", None, "slab", None), P("ens"), P())
    out_specs = P("ens", None, "slab", None)

    def run(ensemble, perturbation, ancestors, bathymetry):
        body = functools.partial(cycle, mesh.shape["ens"], mesh.shape["slab"]) if fits(mesh, ensemble) else shards
        mapped = jax.shard_map(body, mesh=mesh, in_specs=in_specs, out_specs=out_specs, check_vma=False)
        return mapped(ensemble, perturbation, ancestors, bathymetry)

    return run
```

```python
import functools

import jax
import jax.numpy as jnp
from jax import lax
from jax.experimental import pallas as pl
from jax.experimental.pallas import tpu as pltpu
from jax.sharding import PartitionSpec as P

STEPS = 3
MESH = pl.DeviceIdType.MESH
STRIP = 8
LANES = 128


RATIO = 0.3
TURNING = 0.03
JITTER = 0.5
SLOPE = RATIO * 0.5


def padded(cells, sides, width):
    for axis, dim in sides:
        count = lax.axis_size(axis)
        ends = count - 1
        head = lax.slice_in_dim(cells, 0, width, axis=dim)
        tail = lax.slice_in_dim(cells, cells.shape[dim] - width, cells.shape[dim], axis=dim)
        cells = jnp.concatenate(
            [
                lax.ppermute(tail, axis, [(i, (i + 1) % count) for i in range(ends)]),
                cells,
                lax.ppermute(head, axis, [((i + 1) % count, i) for i in range(ends)]),
            ],
            axis=dim,
        )
    return cells


def eastward_difference(field):
    return (jnp.roll(field, -1, -1) - jnp.roll(field, 1, -1)) * 0.5


def step_rows(height, east_vel, north_vel, ocean_floor, inside):
    flux_east = ocean_floor * east_vel
    flux_north = ocean_floor * north_vel
    height_next = height[1:-1] - RATIO * (
        eastward_difference(flux_east[1:-1]) + (flux_north[2:] - flux_north[:-2]) * 0.5
    )
    height_next = jnp.where(inside[1:-1], height_next, 0.0)
    east_next = (
        east_vel[2:-2] - RATIO * eastward_difference(height_next[1:-1]) + TURNING * north_vel[2:-2]
    )
    north_next = (
        north_vel[2:-2]
        - RATIO * (height_next[2:] - height_next[:-2]) * 0.5
        - TURNING * east_vel[2:-2]
    )
    kept = inside[2:-2]
    return (height_next[1:-1], jnp.where(kept, east_next, 0.0), jnp.where(kept, north_next, 0.0))


def edge_rows(members, depth):
    return jnp.stack(
        [jnp.concatenate([member[:depth], member[-depth:]], axis=0) for member in members]
    )


def attach_rims(members, rims, depth):
    return [
        jnp.concatenate([rims[k, :depth], members[k], rims[k, 3 * depth :]], axis=0)
        for k in range(len(members))
    ]


def pick_rows(portion, lineage):
    return jnp.take(portion, lineage, axis=0, mode="clip")


def shards(ensemble, perturbation, ancestors, bathymetry):
    row_count = ensemble.shape[2]
    col_count = ensemble.shape[3]
    total_rows = bathymetry.shape[0]
    first_row = lax.axis_index("slab") * row_count
    widest = 2 * STEPS
    seabed_all = jnp.pad(bathymetry.astype(jnp.float32) * 0.01, ((widest, widest), (0, 0)))
    members = [ensemble[0, 0], ensemble[0, 1], ensemble[0, 2]]
    ocean_floor = lax.dynamic_slice_in_dim(seabed_all, first_row + widest - 2, row_count + 2 * 2, 0)
    global_row = first_row - 2 + jnp.arange(row_count + 2 * 2, dtype=jnp.int32)
    inside = ((global_row >= 0) & (global_row < total_rows))[:, None]
    ocean_floor, inside = (ocean_floor, inside)
    for substep in range(STEPS):
        rims = padded(edge_rows(members, 2), (("slab", 1),), 2)
        widened = attach_rims(members, rims, 2)
        members = list(step_rows(widened[0], widened[1], widened[2], ocean_floor, inside))
    noise = [perturbation[0, 0], perturbation[0, 1], perturbation[0, 2]]
    noise_rims = padded(edge_rows(noise, 1), (("slab", 1),), 1)
    bordered = attach_rims(noise, noise_rims, 1)
    smoothed = jnp.stack(
        [
            (
                4.0 * cell[1:-1]
                + cell[2:]
                + cell[:-2]
                + jnp.roll(cell[1:-1], 1, -1)
                + jnp.roll(cell[1:-1], -1, -1)
            )
            * 0.125
            for cell in bordered
        ]
    )
    lineage = lax.all_gather(ancestors, "ens", axis=0, tiled=True)
    flattened = jnp.stack(members).reshape(1, 3, row_count * col_count)
    pieces = lax.all_to_all(flattened, "ens", split_axis=2, concat_axis=0, tiled=True)
    picked = pick_rows(pieces, lineage)
    returned = lax.all_to_all(picked, "ens", split_axis=0, concat_axis=2, tiled=True)
    selected_parents = returned.reshape(1, 3, row_count, col_count)
    return selected_parents + JITTER * smoothed[None]


def whole_wait(ref, sem):
    pltpu.make_async_copy(ref, ref, sem).wait()


def cycle_kernel(
    n, pair, rows, cols,
    ens_ref, pert_ref, anc_ref, bath_ref, out_ref,
    state, noise, sb, flux, seam, seam_sb, seam_flux, bath_v, pieces0, pieces1, pieces2, picked, res, lin_v, lin_s,
    halo_send, halo_recv, lin_send, lin_recv, lin_local, loads,
    a_send, a_recv, b_send, b_recv,
):
    me = lax.axis_index("ens")
    s = lax.axis_index("slab")
    plane = pair * pair
    line = n // plane
    hubs = 2 * plane
    base = (line // 2 - 1) * plane
    z = me // plane
    y = me // pair % pair
    x = me % pair
    inward = 1 - 2 * (z // (line // 2))
    hub = jnp.logical_and(me >= base, me < base + hubs)
    pieces = (pieces0, pieces1, pieces2)
    top = STRIP
    bottom = STRIP + rows
    barrier = pltpu.get_barrier_semaphore()

    def on(level, k):
        return (level * pair + (y + k // pair) % pair) * pair + (x + k % pair) % pair

    inner = pl.multiple_of((1 - s) * (rows - 2 * STRIP), STRIP)
    fills = [
        pltpu.make_async_copy(src, dst, loads.at[i])
        for i, (src, dst) in enumerate(
            (
                (bath_ref.at[pl.ds(pl.multiple_of(s * (rows - STRIP), STRIP), rows + STRIP)], bath_v),
                (ens_ref, state.at[:, pl.ds(top, rows)]),
                (
                    ens_ref.at[:, pl.ds(inner, 2 * STRIP)],
                    seam.at[:, pl.ds(pl.multiple_of(s * STRIP, STRIP), 2 * STRIP)],
                ),
                (pert_ref, noise.at[:, pl.ds(top, rows)]),
            )
        )
    ]
    for fill in fills:
        fill.start()
    @pl.when(hub)
    def _():
        side = line // 2 - 1 + z // (line // 2)
        for level in (side + inward, side, side - inward, side + 2 * inward):
            for k in reversed(range(plane)):
                to = on(level, k)
                if level is not side or k:
                    pl.semaphore_signal(barrier, inc=1, device_id={"ens": to}, device_id_type=MESH)

    pl.semaphore_signal(barrier, inc=1, device_id={"slab": 1 - s}, device_id_type=MESH)


    lin_v[me] = jnp.full((1, LANES), anc_ref[0], jnp.int32)
    zeros = jnp.zeros((STRIP, cols), jnp.float32)
    for r in (0, bottom):
        flux[r : r + STRIP] = zeros
        state[0, r : r + STRIP] = zeros
    fills[0].wait()
    for r in range(0, rows, STRIP):
        depth = bath_v[pl.ds(pl.multiple_of(s * STRIP + r, STRIP), STRIP)]
        sb[top + r : top + r + STRIP] = depth.astype(jnp.float32) * (0.01 * SLOPE)
    for r in range(0, 3 * STRIP, STRIP):
        depth = bath_v[pl.ds(pl.multiple_of((1 - s) * (rows - 2 * STRIP) + r, STRIP), STRIP)]
        seam_sb[r : r + STRIP] = depth.astype(jnp.float32) * (0.01 * SLOPE)
    fills[1].wait()
    fills[2].wait()

    def east(x):
        return pltpu.roll(x, cols - 1, 1) - pltpu.roll(x, 1, 1)

    def north(ref, r):
        above = ref.shape[0] - STRIP
        up = ref[r + 1 : r + 1 + STRIP] if r < above else pltpu.roll(ref[r : r + STRIP], STRIP - 1, 0)
        down = ref[r - 1 : r - 1 + STRIP] if r else pltpu.roll(ref[r : r + STRIP], 1, 0)
        return up - down

    def fluxes(cells, floor, flow, r):
        here = slice(r, r + STRIP)
        flow[here] = floor[here] * cells[2, here]

    def heights(cells, floor, flow, r):
        here = slice(r, r + STRIP)
        cells[0, here] = cells[0, here] - (east(floor[here] * cells[1, here]) + north(flow, r))

    def velocities(cells, floor, flow, r, last):
        here = slice(r, r + STRIP)
        u = cells[1, here]
        v = cells[2, here]
        h = cells.at[0]
        cells[1, here] = u - SLOPE * east(h[here]) + TURNING * v
        v = v - SLOPE * north(h, r) - TURNING * u
        cells[2, here] = v
        if not last:
            flow[here] = floor[here] * v

    for r in range(top, bottom, STRIP):
        fluxes(state, sb, flux, r)

    def sweep(first, past):
        for wave in range(first, past):
            for step in range(STEPS):
                r = top + (wave - 2 * step) * STRIP
                if top <= r < bottom:
                    heights(state, sb, flux, r)
                if top <= r - STRIP < bottom:
                    velocities(state, sb, flux, r - STRIP, step == STEPS - 1)

    half = plane + 2 * (STEPS - 1)
    early = z >= line // 2
    sweep(0, half)
    pl.when(jnp.logical_not(early))(lambda: sweep(half, half + plane + 1))

    edge = pl.multiple_of((1 - s) * (rows - STRIP), STRIP)

    def strip(ref, f, q, offset):
        return ref.at[f, pl.ds(pl.multiple_of(offset + q * STRIP, STRIP), STRIP)]

    def deliver(f, to):
        pltpu.make_async_remote_copy(
            src_ref=strip(state, f, to - base, top),
            dst_ref=pieces[f].at[me],
            send_sem=a_send.at[f],
            recv_sem=a_recv.at[f],
            device_id={"ens": to},
            device_id_type=MESH,
        ).start()

    def keep(f):
        pltpu.make_async_copy(strip(state, f, me - base, top), pieces[f].at[me], a_recv.at[f]).start()

    def tell(to):
        pltpu.make_async_remote_copy(
            src_ref=lin_v.at[me],
            dst_ref=lin_v.at[me],
            send_sem=lin_send,
            recv_sem=lin_recv,
            device_id={"ens": to},
            device_id_type=MESH,
        ).start()

    side = line // 2 - 1 + z // (line // 2)
    targets = [on(side + inward, k) for k in reversed(range(plane))]
    targets += [on(side, k) for k in reversed(range(plane))]
    seam_hub = base + (1 - s) * (hubs - 1)

    def across(f):
        for to in targets[:plane]:
            pl.when(to != seam_hub)(lambda to=to: deliver(f, to))

    def along(f):
        for to in targets[plane:-1]:
            pl.when(to != seam_hub)(lambda to=to: deliver(f, to))
        to = targets[-1]
        pl.when(jnp.logical_and(jnp.logical_not(hub), to != seam_hub))(lambda: deliver(f, to))
        pl.when(jnp.logical_and(hub, to != seam_hub))(lambda: keep(f))

    def seamed(f):
        pl.when(me != seam_hub)(lambda: deliver(f, seam_hub))
        pl.when(me == seam_hub)(lambda: keep(f))

    pl.semaphore_wait(barrier, hubs + 1 - hub.astype(jnp.int32))
    halos = []
    for i, (src, dst, row) in enumerate(
        ((ens_ref, seam, s * 2 * STRIP), (pert_ref, noise, s * (rows + STRIP)))
    ):
        copy = pltpu.make_async_remote_copy(
            src_ref=src.at[:, pl.ds(edge, STRIP)],
            dst_ref=dst.at[:, pl.ds(pl.multiple_of(row, STRIP), STRIP)],
            send_sem=halo_send.at[i],
            recv_sem=halo_recv.at[i],
            device_id={"slab": 1 - s},
            device_id_type=MESH,
        )
        copy.start()
        halos.append(copy)
    for to in targets[:-1]:
        tell(to)
    pl.when(jnp.logical_not(hub))(lambda: tell(targets[-1]))
    @pl.when(early)
    def _():
        across(0)
        sweep(half, half + plane + 1)

    pl.when(jnp.logical_not(early))(lambda: across(0))
    along(0)
    across(1)
    halos[0].wait()
    for r in range(0, 3 * STRIP, STRIP):
        fluxes(seam, seam_sb, seam_flux, r)
    for step in range(STEPS):
        last = step == STEPS - 1
        for r in range(0, 3 * STRIP, STRIP):
            heights(seam, seam_sb, seam_flux, r)
        for r in range(STRIP, 2 * STRIP, STRIP) if last else range(0, 3 * STRIP, STRIP):
            velocities(seam, seam_sb, seam_flux, r, last)
    for f in range(3):
        state[f, pl.ds(pl.multiple_of(top + edge, STRIP), STRIP)] = seam[f, STRIP : 2 * STRIP]

    seamed(0)
    along(1)
    seamed(1)
    across(2)
    along(2)
    seamed(2)

    wall = pl.multiple_of(s * (rows + STRIP), STRIP)
    for f in range(3):
        noise[f, pl.ds(wall, STRIP)] = zeros
    fills[3].wait()
    halos[1].wait()
    for f in range(3):
        for r in range(top, bottom, STRIP):
            p = noise[f, r : r + STRIP]
            around = noise[f, r + 1 : r + 1 + STRIP] + noise[f, r - 1 : r - 1 + STRIP]
            total = 4.0 * p + around + pltpu.roll(p, 1, 1) + pltpu.roll(p, cols - 1, 1)
            out_ref[f, r - top : r - top + STRIP] = total * 0.125 * JITTER

    order = [t for t in range(line // 2, -(line // 2), -1) if t] + [0]
    spots = [(t, k) for t in order for k in reversed(range(plane))][: n - 1]

    def serve():
        whole_wait(lin_v.at[pl.ds(0, n - 1)], lin_recv)
        fetch = pltpu.make_async_copy(lin_v, lin_s, lin_local)
        fetch.start()
        fetch.wait()

        def reply(f, i):
            t, k = spots[i]
            to = on(z + t * inward, k)
            picked[f, i] = pieces[f][lin_s[to, 0, 0]]
            pltpu.make_async_remote_copy(
                src_ref=picked.at[f, i],
                dst_ref=strip(res, f, me - base, 0),
                send_sem=b_send.at[f],
                recv_sem=b_recv.at[f],
                device_id={"ens": to},
                device_id_type=MESH,
            ).start()

        for stage in range(3 + line // 2):
            if stage < 3:
                whole_wait(pieces[stage], a_recv.at[stage])
            def batch(order, lag, stage=stage):
                for t in order:
                    f = stage - lag[t]
                    for i, (level, k) in enumerate(spots):
                        if level == t and 0 <= f < 3 and (f < 1 or level != 1):
                            reply(f, i)

            pl.when(s == 0)(lambda: batch([2, 1, -1, 0], {2: 0, 1: 1, -1: 0, 0: 0}))
            pl.when(s == 1)(lambda: batch([-1, 0, 2, 1], {2: 1, 1: 2, -1: 0, 0: 0}))
            if stage < 3:
                picked[stage, n - 1] = pieces[stage][lin_s[me, 0, 0]]
                pltpu.make_async_copy(
                    picked.at[stage, n - 1], strip(res, stage, me - base, 0), b_recv.at[stage]
                ).start()

        for i, (level, k) in enumerate(spots):
            for f in (1, 2):
                if level == 1:
                    reply(f, i)

    pl.when(hub)(serve)

    for f in range(3):
        whole_wait(res.at[f], b_recv.at[f])
        for r in range(0, rows, STRIP):
            out_ref[f, r : r + STRIP] = res[f, r : r + STRIP] + out_ref[f, r : r + STRIP]

    @pl.when(hub)
    def _():
        whole_wait(lin_v.at[pl.ds(0, hubs - 1)], lin_send)
        for f in range(3):
            whole_wait(pieces[f].at[pl.ds(0, hubs - 1)], a_send.at[f])
            whole_wait(picked.at[f, pl.ds(0, n - 1)], b_send.at[f])

    @pl.when(jnp.logical_not(hub))
    def _():
        whole_wait(lin_v.at[pl.ds(0, hubs)], lin_send)
        for f in range(3):
            whole_wait(pieces[f].at[pl.ds(0, hubs)], a_send.at[f])


def cycle(n, pair, ensemble, perturbation, ancestors, bathymetry):
    rows, cols = ensemble.shape[2:]
    tall = rows + 2 * STRIP
    f32 = jnp.float32
    vmem = pl.BlockSpec(memory_space=pltpu.VMEM)
    hbm = pl.BlockSpec(memory_space=pltpu.HBM)
    dma = pltpu.SemaphoreType.DMA
    held = [
        pltpu.with_memory_space_constraint(x, pltpu.HBM)
        for x in (ensemble[0], perturbation[0], bathymetry)
    ]
    result = pl.pallas_call(
        functools.partial(cycle_kernel, n, pair, rows, cols),
        out_shape=jax.ShapeDtypeStruct((3, rows, cols), f32),
        in_specs=[hbm, hbm, pl.BlockSpec(memory_space=pltpu.SMEM), hbm],
        out_specs=vmem,
        scratch_shapes=[
            pltpu.VMEM((3, tall, cols), f32),
            pltpu.VMEM((3, tall, cols), f32),
            pltpu.VMEM((tall, cols), f32),
            pltpu.VMEM((tall, cols), f32),
            pltpu.VMEM((3, 3 * STRIP, cols), f32),
            pltpu.VMEM((3 * STRIP, cols), f32),
            pltpu.VMEM((3 * STRIP, cols), f32),
            pltpu.VMEM((rows + STRIP, cols), jnp.int32),
            pltpu.VMEM((n, STRIP, cols), f32),
            pltpu.VMEM((n, STRIP, cols), f32),
            pltpu.VMEM((n, STRIP, cols), f32),
            pltpu.VMEM((3, n, STRIP, cols), f32),
            pltpu.VMEM((3, rows, cols), f32),
            pltpu.VMEM((n, 1, LANES), jnp.int32),
            pltpu.SMEM((n, 1, LANES), jnp.int32),
            dma((2,)), dma((2,)), dma(()), dma(()), dma(()), dma((4,)),
            dma((3,)), dma((3,)), dma((3,)), dma((3,)),
        ],
        compiler_params=pltpu.CompilerParams(collective_id=0, has_side_effects=True, vmem_limit_bytes=24 << 20),
        name="cycle",
    )(*held[:2], ancestors, held[2])
    return result[None]


def fits(mesh, ensemble):
    n, slabs = mesh.shape["ens"], mesh.shape["slab"]
    plane = slabs * slabs
    rows, cols = ensemble.shape[2] // slabs, ensemble.shape[3]
    if slabs != 2 or ensemble.shape[0] != n or n != plane * plane:
        return False
    return rows == 2 * plane * STRIP and cols % LANES == 0


def solution(mesh):
    in_specs = (P("ens", None, "slab", None), P("ens", None, "slab", None), P("ens"), P())
    out_specs = P("ens", None, "slab", None)

    def run(ensemble, perturbation, ancestors, bathymetry):
        body = functools.partial(cycle, mesh.shape["ens"], mesh.shape["slab"]) if fits(mesh, ensemble) else shards
        mapped = jax.shard_map(body, mesh=mesh, in_specs=in_specs, out_specs=out_specs, check_vma=False)
        return mapped(ensemble, perturbation, ancestors, bathymetry)

    return run
```

```python
import functools

import jax
import jax.numpy as jnp
from jax import lax
from jax.experimental import pallas as pl
from jax.experimental.pallas import tpu as pltpu
from jax.sharding import PartitionSpec as P

STEPS = 3
MESH = pl.DeviceIdType.MESH
STRIP = 8
LANES = 128


RATIO = 0.3
TURNING = 0.03
JITTER = 0.5
SLOPE = RATIO * 0.5


def padded(cells, sides, width):
    for axis, dim in sides:
        count = lax.axis_size(axis)
        ends = count - 1
        head = lax.slice_in_dim(cells, 0, width, axis=dim)
        tail = lax.slice_in_dim(cells, cells.shape[dim] - width, cells.shape[dim], axis=dim)
        cells = jnp.concatenate(
            [
                lax.ppermute(tail, axis, [(i, (i + 1) % count) for i in range(ends)]),
                cells,
                lax.ppermute(head, axis, [((i + 1) % count, i) for i in range(ends)]),
            ],
            axis=dim,
        )
    return cells


def eastward_difference(field):
    return (jnp.roll(field, -1, -1) - jnp.roll(field, 1, -1)) * 0.5


def step_rows(height, east_vel, north_vel, ocean_floor, inside):
    flux_east = ocean_floor * east_vel
    flux_north = ocean_floor * north_vel
    height_next = height[1:-1] - RATIO * (
        eastward_difference(flux_east[1:-1]) + (flux_north[2:] - flux_north[:-2]) * 0.5
    )
    height_next = jnp.where(inside[1:-1], height_next, 0.0)
    east_next = (
        east_vel[2:-2] - RATIO * eastward_difference(height_next[1:-1]) + TURNING * north_vel[2:-2]
    )
    north_next = (
        north_vel[2:-2]
        - RATIO * (height_next[2:] - height_next[:-2]) * 0.5
        - TURNING * east_vel[2:-2]
    )
    kept = inside[2:-2]
    return (height_next[1:-1], jnp.where(kept, east_next, 0.0), jnp.where(kept, north_next, 0.0))


def edge_rows(members, depth):
    return jnp.stack(
        [jnp.concatenate([member[:depth], member[-depth:]], axis=0) for member in members]
    )


def attach_rims(members, rims, depth):
    return [
        jnp.concatenate([rims[k, :depth], members[k], rims[k, 3 * depth :]], axis=0)
        for k in range(len(members))
    ]


def pick_rows(portion, lineage):
    return jnp.take(portion, lineage, axis=0, mode="clip")


def shards(ensemble, perturbation, ancestors, bathymetry):
    row_count = ensemble.shape[2]
    col_count = ensemble.shape[3]
    total_rows = bathymetry.shape[0]
    first_row = lax.axis_index("slab") * row_count
    widest = 2 * STEPS
    seabed_all = jnp.pad(bathymetry.astype(jnp.float32) * 0.01, ((widest, widest), (0, 0)))
    members = [ensemble[0, 0], ensemble[0, 1], ensemble[0, 2]]
    ocean_floor = lax.dynamic_slice_in_dim(seabed_all, first_row + widest - 2, row_count + 2 * 2, 0)
    global_row = first_row - 2 + jnp.arange(row_count + 2 * 2, dtype=jnp.int32)
    inside = ((global_row >= 0) & (global_row < total_rows))[:, None]
    ocean_floor, inside = (ocean_floor, inside)
    for substep in range(STEPS):
        rims = padded(edge_rows(members, 2), (("slab", 1),), 2)
        widened = attach_rims(members, rims, 2)
        members = list(step_rows(widened[0], widened[1], widened[2], ocean_floor, inside))
    noise = [perturbation[0, 0], perturbation[0, 1], perturbation[0, 2]]
    noise_rims = padded(edge_rows(noise, 1), (("slab", 1),), 1)
    bordered = attach_rims(noise, noise_rims, 1)
    smoothed = jnp.stack(
        [
            (
                4.0 * cell[1:-1]
                + cell[2:]
                + cell[:-2]
                + jnp.roll(cell[1:-1], 1, -1)
                + jnp.roll(cell[1:-1], -1, -1)
            )
            * 0.125
            for cell in bordered
        ]
    )
    lineage = lax.all_gather(ancestors, "ens", axis=0, tiled=True)
    flattened = jnp.stack(members).reshape(1, 3, row_count * col_count)
    pieces = lax.all_to_all(flattened, "ens", split_axis=2, concat_axis=0, tiled=True)
    picked = pick_rows(pieces, lineage)
    returned = lax.all_to_all(picked, "ens", split_axis=0, concat_axis=2, tiled=True)
    selected_parents = returned.reshape(1, 3, row_count, col_count)
    return selected_parents + JITTER * smoothed[None]


def whole_wait(ref, sem):
    pltpu.make_async_copy(ref, ref, sem).wait()


def cycle_kernel(
    n, pair, rows, cols,
    ens_ref, pert_ref, anc_ref, bath_ref, out_ref,
    state, noise, sb, flux, seam, seam_sb, seam_flux, bath_v, pieces0, pieces1, pieces2, picked, res, lin_v, lin_s,
    halo_send, halo_recv, lin_send, lin_recv, lin_local, loads,
    a_send, a_recv, b_send, b_recv,
):
    me = lax.axis_index("ens")
    s = lax.axis_index("slab")
    plane = pair * pair
    line = n // plane
    hubs = 2 * plane
    base = (line // 2 - 1) * plane
    z = me // plane
    y = me // pair % pair
    x = me % pair
    inward = 1 - 2 * (z // (line // 2))
    hub = jnp.logical_and(me >= base, me < base + hubs)
    pieces = (pieces0, pieces1, pieces2)
    top = STRIP
    bottom = STRIP + rows
    barrier = pltpu.get_barrier_semaphore()

    def on(level, k):
        return (level * pair + (y + k // pair) % pair) * pair + (x + k % pair) % pair

    inner = pl.multiple_of((1 - s) * (rows - 2 * STRIP), STRIP)
    fills = [
        pltpu.make_async_copy(src, dst, loads.at[i])
        for i, (src, dst) in enumerate(
            (
                (bath_ref.at[pl.ds(pl.multiple_of(s * (rows - STRIP), STRIP), rows + STRIP)], bath_v),
                (ens_ref, state.at[:, pl.ds(top, rows)]),
                (
                    ens_ref.at[:, pl.ds(inner, 2 * STRIP)],
                    seam.at[:, pl.ds(pl.multiple_of(s * STRIP, STRIP), 2 * STRIP)],
                ),
                (pert_ref, noise.at[:, pl.ds(top, rows)]),
            )
        )
    ]
    for fill in fills:
        fill.start()
    @pl.when(hub)
    def _():
        side = line // 2 - 1 + z // (line // 2)
        for level in (side + inward, side, side - inward, side + 2 * inward):
            for k in reversed(range(plane)):
                to = on(level, k)
                if level is not side or k:
                    pl.semaphore_signal(barrier, inc=1, device_id={"ens": to}, device_id_type=MESH)

    pl.semaphore_signal(barrier, inc=1, device_id={"slab": 1 - s}, device_id_type=MESH)


    lin_v[me] = jnp.full((1, LANES), anc_ref[0], jnp.int32)
    zeros = jnp.zeros((STRIP, cols), jnp.float32)
    for r in (0, bottom):
        flux[r : r + STRIP] = zeros
        state[0, r : r + STRIP] = zeros
    fills[0].wait()
    for r in range(0, rows, STRIP):
        depth = bath_v[pl.ds(pl.multiple_of(s * STRIP + r, STRIP), STRIP)]
        sb[top + r : top + r + STRIP] = depth.astype(jnp.float32) * (0.01 * SLOPE)
    for r in range(0, 3 * STRIP, STRIP):
        depth = bath_v[pl.ds(pl.multiple_of((1 - s) * (rows - 2 * STRIP) + r, STRIP), STRIP)]
        seam_sb[r : r + STRIP] = depth.astype(jnp.float32) * (0.01 * SLOPE)
    fills[1].wait()
    fills[2].wait()

    def east(x):
        return pltpu.roll(x, cols - 1, 1) - pltpu.roll(x, 1, 1)

    def north(ref, r):
        above = ref.shape[0] - STRIP
        up = ref[r + 1 : r + 1 + STRIP] if r < above else pltpu.roll(ref[r : r + STRIP], STRIP - 1, 0)
        down = ref[r - 1 : r - 1 + STRIP] if r else pltpu.roll(ref[r : r + STRIP], 1, 0)
        return up - down

    def fluxes(cells, floor, flow, r):
        here = slice(r, r + STRIP)
        flow[here] = floor[here] * cells[2, here]

    def heights(cells, floor, flow, r):
        here = slice(r, r + STRIP)
        cells[0, here] = cells[0, here] - (east(floor[here] * cells[1, here]) + north(flow, r))

    def velocities(cells, floor, flow, r, last):
        here = slice(r, r + STRIP)
        u = cells[1, here]
        v = cells[2, here]
        h = cells.at[0]
        cells[1, here] = u - SLOPE * east(h[here]) + TURNING * v
        v = v - SLOPE * north(h, r) - TURNING * u
        cells[2, here] = v
        if not last:
            flow[here] = floor[here] * v

    for r in range(top, bottom, STRIP):
        fluxes(state, sb, flux, r)

    def sweep(first, past):
        for wave in range(first, past):
            for step in range(STEPS):
                r = top + (wave - 2 * step) * STRIP
                if top <= r < bottom:
                    heights(state, sb, flux, r)
                if top <= r - STRIP < bottom:
                    velocities(state, sb, flux, r - STRIP, step == STEPS - 1)

    half = plane + 2 * (STEPS - 1)
    early = z >= line // 2
    sweep(0, half)
    pl.when(jnp.logical_not(early))(lambda: sweep(half, half + plane + 1))

    edge = pl.multiple_of((1 - s) * (rows - STRIP), STRIP)

    def strip(ref, f, q, offset):
        return ref.at[f, pl.ds(pl.multiple_of(offset + q * STRIP, STRIP), STRIP)]

    def deliver(f, to):
        pltpu.make_async_remote_copy(
            src_ref=strip(state, f, to - base, top),
            dst_ref=pieces[f].at[me],
            send_sem=a_send.at[f],
            recv_sem=a_recv.at[f],
            device_id={"ens": to},
            device_id_type=MESH,
        ).start()

    def keep(f):
        pltpu.make_async_copy(strip(state, f, me - base, top), pieces[f].at[me], a_recv.at[f]).start()

    def tell(to):
        pltpu.make_async_remote_copy(
            src_ref=lin_v.at[me],
            dst_ref=lin_v.at[me],
            send_sem=lin_send,
            recv_sem=lin_recv,
            device_id={"ens": to},
            device_id_type=MESH,
        ).start()

    side = line // 2 - 1 + z // (line // 2)
    targets = [on(side + inward, k) for k in reversed(range(plane))]
    targets += [on(side, k) for k in reversed(range(plane))]
    seam_hub = base + (1 - s) * (hubs - 1)

    def across(f):
        for to in targets[:plane]:
            pl.when(to != seam_hub)(lambda to=to: deliver(f, to))

    def along(f):
        for to in targets[plane:-1]:
            pl.when(to != seam_hub)(lambda to=to: deliver(f, to))
        to = targets[-1]
        pl.when(jnp.logical_and(jnp.logical_not(hub), to != seam_hub))(lambda: deliver(f, to))
        pl.when(jnp.logical_and(hub, to != seam_hub))(lambda: keep(f))

    def seamed(f):
        pl.when(me != seam_hub)(lambda: deliver(f, seam_hub))
        pl.when(me == seam_hub)(lambda: keep(f))

    pl.semaphore_wait(barrier, hubs + 1 - hub.astype(jnp.int32))
    halos = []
    for i, (src, dst, row) in enumerate(
        ((ens_ref, seam, s * 2 * STRIP), (pert_ref, noise, s * (rows + STRIP)))
    ):
        copy = pltpu.make_async_remote_copy(
            src_ref=src.at[:, pl.ds(edge, STRIP)],
            dst_ref=dst.at[:, pl.ds(pl.multiple_of(row, STRIP), STRIP)],
            send_sem=halo_send.at[i],
            recv_sem=halo_recv.at[i],
            device_id={"slab": 1 - s},
            device_id_type=MESH,
        )
        copy.start()
        halos.append(copy)
    for to in targets[:-1]:
        tell(to)
    pl.when(jnp.logical_not(hub))(lambda: tell(targets[-1]))
    @pl.when(early)
    def _():
        across(0)
        sweep(half, half + plane + 1)

    pl.when(jnp.logical_not(early))(lambda: across(0))
    along(0)
    across(1)
    halos[0].wait()
    for r in range(0, 3 * STRIP, STRIP):
        fluxes(seam, seam_sb, seam_flux, r)
    for step in range(STEPS):
        last = step == STEPS - 1
        for r in range(0, 3 * STRIP, STRIP):
            heights(seam, seam_sb, seam_flux, r)
        for r in range(STRIP, 2 * STRIP, STRIP) if last else range(0, 3 * STRIP, STRIP):
            velocities(seam, seam_sb, seam_flux, r, last)
    for f in range(3):
        state[f, pl.ds(pl.multiple_of(top + edge, STRIP), STRIP)] = seam[f, STRIP : 2 * STRIP]

    seamed(0)
    along(1)
    seamed(1)
    across(2)
    along(2)
    seamed(2)

    wall = pl.multiple_of(s * (rows + STRIP), STRIP)
    for f in range(3):
        noise[f, pl.ds(wall, STRIP)] = zeros
    fills[3].wait()
    halos[1].wait()
    for f in range(3):
        for r in range(top, bottom, STRIP):
            p = noise[f, r : r + STRIP]
            around = noise[f, r + 1 : r + 1 + STRIP] + noise[f, r - 1 : r - 1 + STRIP]
            total = 4.0 * p + around + pltpu.roll(p, 1, 1) + pltpu.roll(p, cols - 1, 1)
            out_ref[f, r - top : r - top + STRIP] = total * 0.125 * JITTER

    order = [t for t in range(line // 2, -(line // 2), -1) if t] + [0]
    spots = [(t, k) for t in order for k in reversed(range(plane))][: n - 1]

    def serve():
        whole_wait(lin_v.at[pl.ds(0, n - 1)], lin_recv)
        fetch = pltpu.make_async_copy(lin_v, lin_s, lin_local)
        fetch.start()
        fetch.wait()

        def reply(f, i):
            t, k = spots[i]
            to = on(z + t * inward, k)
            picked[f, i] = pieces[f][lin_s[to, 0, 0]]
            pltpu.make_async_remote_copy(
                src_ref=picked.at[f, i],
                dst_ref=strip(res, f, me - base, 0),
                send_sem=b_send.at[f],
                recv_sem=b_recv.at[f, (me - base) // plane],
                device_id={"ens": to},
                device_id_type=MESH,
            ).start()

        for stage in range(3 + line // 2):
            if stage < 3:
                whole_wait(pieces[stage], a_recv.at[stage])
            def batch(order, lag, stage=stage):
                for t in order:
                    f = stage - lag[t]
                    for i, (level, k) in enumerate(spots):
                        if level == t and 0 <= f < 3 and (f < 1 or level != 1):
                            reply(f, i)

            pl.when(s == 0)(lambda: batch([2, 1, -1, 0], {2: 0, 1: 1, -1: 0, 0: 0}))
            pl.when(s == 1)(lambda: batch([-1, 0, 2, 1], {2: 1, 1: 2, -1: 0, 0: 0}))
            if stage < 3:
                picked[stage, n - 1] = pieces[stage][lin_s[me, 0, 0]]
                pltpu.make_async_copy(
                    picked.at[stage, n - 1], strip(res, stage, me - base, 0), b_recv.at[stage, (me - base) // plane]
                ).start()

        for i, (level, k) in enumerate(spots):
            for f in (1, 2):
                if level == 1:
                    reply(f, i)

    pl.when(hub)(serve)

    near = z // (line // 2)
    for f in range(3):
        for half in (near, 1 - near):
            start = half * plane * STRIP
            whole_wait(res.at[f, pl.ds(pl.multiple_of(start, STRIP), plane * STRIP)], b_recv.at[f, half])
            for q in range(plane):
                here = pl.ds(pl.multiple_of(start + q * STRIP, STRIP), STRIP)
                out_ref[f, here] = res[f, here] + out_ref[f, here]

    @pl.when(hub)
    def _():
        whole_wait(lin_v.at[pl.ds(0, hubs - 1)], lin_send)
        for f in range(3):
            whole_wait(pieces[f].at[pl.ds(0, hubs - 1)], a_send.at[f])
            whole_wait(picked.at[f, pl.ds(0, n - 1)], b_send.at[f])

    @pl.when(jnp.logical_not(hub))
    def _():
        whole_wait(lin_v.at[pl.ds(0, hubs)], lin_send)
        for f in range(3):
            whole_wait(pieces[f].at[pl.ds(0, hubs)], a_send.at[f])


def cycle(n, pair, ensemble, perturbation, ancestors, bathymetry):
    rows, cols = ensemble.shape[2:]
    tall = rows + 2 * STRIP
    f32 = jnp.float32
    vmem = pl.BlockSpec(memory_space=pltpu.VMEM)
    hbm = pl.BlockSpec(memory_space=pltpu.HBM)
    dma = pltpu.SemaphoreType.DMA
    held = [
        pltpu.with_memory_space_constraint(x, pltpu.HBM)
        for x in (ensemble[0], perturbation[0], bathymetry)
    ]
    result = pl.pallas_call(
        functools.partial(cycle_kernel, n, pair, rows, cols),
        out_shape=jax.ShapeDtypeStruct((3, rows, cols), f32),
        in_specs=[hbm, hbm, pl.BlockSpec(memory_space=pltpu.SMEM), hbm],
        out_specs=vmem,
        scratch_shapes=[
            pltpu.VMEM((3, tall, cols), f32),
            pltpu.VMEM((3, tall, cols), f32),
            pltpu.VMEM((tall, cols), f32),
            pltpu.VMEM((tall, cols), f32),
            pltpu.VMEM((3, 3 * STRIP, cols), f32),
            pltpu.VMEM((3 * STRIP, cols), f32),
            pltpu.VMEM((3 * STRIP, cols), f32),
            pltpu.VMEM((rows + STRIP, cols), jnp.int32),
            pltpu.VMEM((n, STRIP, cols), f32),
            pltpu.VMEM((n, STRIP, cols), f32),
            pltpu.VMEM((n, STRIP, cols), f32),
            pltpu.VMEM((3, n, STRIP, cols), f32),
            pltpu.VMEM((3, rows, cols), f32),
            pltpu.VMEM((n, 1, LANES), jnp.int32),
            pltpu.SMEM((n, 1, LANES), jnp.int32),
            dma((2,)), dma((2,)), dma(()), dma(()), dma(()), dma((4,)),
            dma((3,)), dma((3,)), dma((3,)), dma((3, 2)),
        ],
        compiler_params=pltpu.CompilerParams(collective_id=0, has_side_effects=True, vmem_limit_bytes=24 << 20),
        name="cycle",
    )(*held[:2], ancestors, held[2])
    return result[None]


def fits(mesh, ensemble):
    n, slabs = mesh.shape["ens"], mesh.shape["slab"]
    plane = slabs * slabs
    rows, cols = ensemble.shape[2] // slabs, ensemble.shape[3]
    if slabs != 2 or ensemble.shape[0] != n or n != plane * plane:
        return False
    return rows == 2 * plane * STRIP and cols % LANES == 0


def solution(mesh):
    in_specs = (P("ens", None, "slab", None), P("ens", None, "slab", None), P("ens"), P())
    out_specs = P("ens", None, "slab", None)

    def run(ensemble, perturbation, ancestors, bathymetry):
        body = functools.partial(cycle, mesh.shape["ens"], mesh.shape["slab"]) if fits(mesh, ensemble) else shards
        mapped = jax.shard_map(body, mesh=mesh, in_specs=in_specs, out_specs=out_specs, check_vma=False)
        return mapped(ensemble, perturbation, ancestors, bathymetry)

    return run
```
